128 devices in a mesh: col: 8 (over y, core), row: 16 (over z, x).
Axes of the slice: x: 4, y: 4, z: 4, core: 2. Of those that a mesh axis runs over, the one named last changes fastest.
Arguments:
- multipoles: float32 [64, 131072], P(None, ('row', 'col')), may hold values from -6 to 6
- parent_locals: float32 [64, 131072], P(None, ('row', 'col')), may hold values from -6 to 6
- operators: float32 [316, 64, 64], replicated, may hold values from -0.125 to 0.125
- pair_target: int32 [316, 16384], P(None, ('row', 'col')), may hold values from 0 to 1023
- pair_partner: int32 [316, 16384], P(None, ('row', 'col')), may hold values from 0 to 9215, as said below
- pair_count: int32 [128, 316], P(('row', 'col')), may hold values from 1 to 128, as said below
- send_cells: int32 [128, 8192], P(('row', 'col')), may hold values from 0 to 1023, as said below
- send_count: int32 [128, 128], P(('row', 'col')), may hold values from 32 to 64, as said below
Outputs:
- locals_out: float32 [64, 131072], P(None, ('row', 'col'))
The draws below stay inside these ranges and needn't reach their ends.
Inputs may be any that keep to these rules, and one draw needn't show every extreme that they name: pair_count[d, k] live pairs stand first in the positions of offset k on device d; some device has 128 live pairs at every offset. send_count[s, d] is the number of live slots, counted from the first, of the 64 slots that device s sends to device d; every device receives 64 live slots from some device. send_cells[s, d * 64 + j] is the local cell of device s in slot j of what it sends to device d; the slots sent to one device name distinct cells. `pair_partner`: A value p below 1024 names a local cell other than the pair's target; a value p at or above names slot (p - 1024) % 64 sent by device (p - 1024) // 64 to the pair's device, and that slot is live.
All inputs are finite; a program needn't handle non-finite values.
Results may differ from the reference program's by a relative error of at most 0.0003.
Values sent between devices are 32-bit elements; how exact they have to be, the bound alone decides.
No kernel may reach another device: no remote copies, remote signals or barrier semaphores. Data moves between devices by JAX's collectives and lax.ppermute only.
A program may use at most 128 MiB of HBM per device.

```python
import jax
import jax.numpy as jnp
from jax import lax

COEF = 64
OFFSETS = 316
CELLS_DEV = 1024
SLOTS = 64
PER = 128
PEERS = 128
CELLS = 131072


def make_plan(key):
    keys = jax.random.split(jax.random.fold_in(key, 7103), 11)
    devices = PEERS
    send_count = jax.random.randint(keys[0], (devices, devices), SLOTS // 2, SLOTS + 1)
    full_source = jax.random.randint(keys[1], (devices,), 0, devices)
    full_source = full_source.at[0].set(devices - 1)
    send_count = jnp.where(jnp.arange(devices)[:, None] == full_source[None, :], SLOTS, send_count)
    cell_stride = CELLS_DEV // SLOTS
    jitter = jax.random.randint(keys[2], (devices, devices, SLOTS), 0, cell_stride)
    send_cells = jnp.arange(SLOTS, dtype=jnp.int32)[None, None, :] * cell_stride + jitter
    send_cells = send_cells.at[0, 0, 0].set(0).at[0, 0, SLOTS - 1].set(CELLS_DEV - 1)
    send_cells = send_cells.reshape(devices, devices * SLOTS)
    load_level = 2 ** jax.random.randint(keys[3], (devices,), 0, 4)
    busiest = jax.random.randint(keys[4], (), 0, devices)
    is_busiest = jnp.arange(devices) == busiest
    load_level = jnp.where(is_busiest, 8, load_level)
    dither = jax.random.randint(keys[5], (devices, OFFSETS), 0, max(PER // 16, 1))
    dither = jnp.where(is_busiest[:, None], 0, dither)
    pair_count = load_level[:, None] * PER // 8 - dither
    shape = (OFFSETS, devices, PER)
    targets = jax.random.randint(keys[6], shape, 0, CELLS_DEV)
    remote_flag = jax.random.randint(keys[7], shape, 0, 2)
    source_device = jax.random.randint(keys[8], shape, 0, devices)
    local_step = jax.random.randint(keys[9], shape, 1, CELLS_DEV)
    raw_bits = jax.random.randint(keys[10], shape, 0, 1 << 20)
    receiver = jnp.arange(devices, dtype=jnp.int32)[None, :, None]
    live_limit = send_count[source_device, receiver]
    slot_pick = raw_bits % live_limit
    local_cell = (targets + local_step) % CELLS_DEV
    partners = jnp.where(remote_flag == 1, CELLS_DEV + source_device * SLOTS + slot_pick, local_cell)
    targets = targets.at[0, 0, 1].set(CELLS_DEV - 1).at[0, 0, 2].set(0).at[0, 0, 3].set(1)
    partners = partners.at[0, 0, 0].set(CELLS_DEV + (devices - 1) * SLOTS + SLOTS - 1)
    partners = partners.at[0, 0, 1].set(CELLS_DEV).at[0, 0, 2].set(CELLS_DEV).at[0, 0, 3].set(0)
    return (targets.reshape(OFFSETS, devices * PER).astype(jnp.int32), partners.reshape(OFFSETS, devices * PER).astype(jnp.int32), pair_count.astype(jnp.int32), send_cells.astype(jnp.int32), send_count.astype(jnp.int32))


def draw_pair_target(key, part):
    return make_plan(key)[0]


def draw_pair_partner(key, part):
    return make_plan(key)[1]


def draw_pair_count(key, part):
    return make_plan(key)[2]


def draw_send_cells(key, part):
    return make_plan(key)[3]


def draw_send_count(key, part):
    return make_plan(key)[4]


def block_scale(own_key, shape, shards, smallest, high):
    factor_of, own = 1.0, jax.random.fold_in(own_key, 6)
    for position, blocks in shards:
        steps = jnp.exp(jax.random.uniform(jax.random.fold_in(own, position), (blocks,), jnp.float32, smallest / len(shards), high / len(shards)))
        factor_of = factor_of * jnp.repeat(steps, shape[position] // blocks).reshape([-1 if axis == position else 1 for axis in range(len(shape))])
    return factor_of


def bell_draw(stream_key, extent, scale, most, cuts=(), held_as=jnp.bfloat16):
    entries = scale * jax.random.normal(stream_key, extent, jnp.float32)
    if cuts:
        entries = entries * block_scale(stream_key, extent, cuts, -0.22, 0.18)
    return jnp.clip(entries, -most, most).astype(held_as)


def setup_inputs(seed: int = 0) -> dict:
    seeds = jax.random.split(jax.random.key(seed), 9)
    return {
        "multipoles": bell_draw(seeds[0], (COEF, CELLS), 1.0, 6.0, ((1, 128),), jnp.float32),
        "parent_locals": bell_draw(seeds[1], (COEF, CELLS), 1.0, 6.0, ((1, 128),), jnp.float32),
        "operators": bell_draw(seeds[2], (OFFSETS, COEF, COEF), (COEF * (OFFSETS * PER // CELLS_DEV + 1)) ** -0.5, 0.125, (), jnp.float32),
        "pair_target": draw_pair_target(jax.random.fold_in(seeds[8], 71), 0),
        "pair_partner": draw_pair_partner(jax.random.fold_in(seeds[8], 71), 0),
        "pair_count": draw_pair_count(jax.random.fold_in(seeds[8], 71), 0),
        "send_cells": draw_send_cells(jax.random.fold_in(seeds[8], 71), 0),
        "send_count": draw_send_count(jax.random.fold_in(seeds[8], 71), 0),
    }


def reference(multipoles, parent_locals, operators, pair_target, pair_partner, pair_count, send_cells, send_count):
    components = multipoles.shape[0]
    reverse = operators[::-1]
    holder_ids = jnp.arange(PEERS, dtype=jnp.int32)
    slot_ids = jnp.arange(SLOTS, dtype=jnp.int32)
    bucket_ids = jnp.arange(PER, dtype=jnp.int32)

    def one_device(summed, device):
        targets = lax.dynamic_slice_in_dim(pair_target, (device * PER).astype(jnp.int32), PER, 1)
        partners = lax.dynamic_slice_in_dim(pair_partner, (device * PER).astype(jnp.int32), PER, 1)
        bucket_counts = lax.dynamic_index_in_dim(pair_count, device, 0, keepdims=False)
        sent_slots = lax.dynamic_slice_in_dim(send_cells, (device * SLOTS).astype(jnp.int32), SLOTS, 1)
        live_limit = lax.dynamic_index_in_dim(send_count, device, 1, keepdims=False)
        fetch_cell = (holder_ids[:, None] * CELLS_DEV + sent_slots).reshape(-1)
        fetch_live = (slot_ids[None, :] < live_limit[:, None]).reshape(-1)
        remote_index = jnp.clip(partners - CELLS_DEV, 0, PEERS * SLOTS - 1)
        is_local = partners < CELLS_DEV
        partner_cell = jnp.where(is_local, device * CELLS_DEV + partners, fetch_cell[remote_index])
        partner_live = jnp.where(is_local, True, fetch_live[remote_index])
        target_cell = device * CELLS_DEV + targets
        pair_live = bucket_ids[None, :] < bucket_counts[:, None]
        pair_weight = pair_live.astype(jnp.float32)
        keep_weight = (pair_live & partner_live).astype(jnp.float32)
        far_side = jnp.take(multipoles, partner_cell, axis=1) * partner_live.astype(jnp.float32)[None]
        target_terms = jnp.take(multipoles, target_cell, axis=1)
        to_target = jnp.einsum("kij,jkp->ikp", operators, far_side, precision=lax.Precision.HIGHEST) * pair_weight[None]
        to_partner = jnp.einsum("kij,jkp->ikp", reverse, target_terms, precision=lax.Precision.HIGHEST) * keep_weight[None]
        summed = summed.at[:, target_cell.reshape(-1)].add(to_target.reshape(components, -1))
        summed = summed.at[:, partner_cell.reshape(-1)].add(to_partner.reshape(components, -1))
        return summed, None

    summed, _ = lax.scan(one_device, parent_locals.astype(jnp.float32), jnp.arange(PEERS, dtype=jnp.int32))
    return summed
```

```python
import functools

import jax
import jax.numpy as jnp
from jax import lax
from jax.experimental import pallas as pl
from jax.experimental.pallas import tpu as pltpu
from jax.sharding import PartitionSpec as P

F32 = jnp.float32
BF16 = jnp.bfloat16

COEF = 64
LANES = 128
CELLS = 1024
REMOTE = 8192
TABLE = CELLS + REMOTE
GROUP = 4
GROUPS = 80
LIVE_GROUPS = 79
ROWS = GROUP * LANES
BANKS = 8
VMEM_LIMIT = 60 * 1024 * 1024


def dot_nn(a, b):
    return lax.dot_general(a, b, (((1,), (0,)), ((), ())), preferred_element_type=F32)


def dot_nt(a, b):
    return lax.dot_general(a, b, (((1,), (1,)), ((), ())), preferred_element_type=F32)


def split(x):
    hi = x.astype(BF16)
    lo = (x - hi.astype(F32)).astype(BF16)
    return hi, lo


def operator_weights(op):
    hi, lo = split(op)
    return jnp.concatenate(
        [jnp.concatenate([hi, hi], axis=1), jnp.concatenate([lo, lo], axis=1)], axis=0
    )


def cell_table(multipoles):
    hi = multipoles.astype(BF16).astype(F32)
    lo = multipoles - hi
    return jnp.concatenate([hi, lo], axis=0).T


def one_hot_rows(index_block, count):
    columns = index_block.T
    cell = lax.broadcasted_iota(jnp.int32, (LANES, CELLS), 1)
    return jnp.concatenate(
        [(columns[:, i : i + 1] == cell).astype(F32).astype(BF16) for i in range(count)], axis=0
    )


def one_hot_columns(index_block, count):
    cell = lax.broadcasted_iota(jnp.int32, (CELLS, LANES), 0)
    return jnp.concatenate(
        [(index_block[i : i + 1, :] == cell).astype(F32).astype(BF16) for i in range(count)], axis=1
    )


def both_halves(x):
    return x + pltpu.roll(x, COEF, 1)


def unpack_rows(packed):
    hi = packed.astype(BF16).astype(F32)
    lo = packed - hi
    left = lax.broadcasted_iota(jnp.int32, packed.shape, packed.ndim - 1) < COEF
    axis = packed.ndim - 1
    first = jnp.where(left, hi, pltpu.roll(lo, COEF, axis))
    second = jnp.where(left, pltpu.roll(hi, COEF, axis), lo)
    return jnp.concatenate([first, second], axis=packed.ndim - 2)


def send_kernel(cells_ref, multipoles_ref, out_ref):
    table = cell_table(multipoles_ref[...]).astype(BF16)
    left = lax.broadcasted_iota(jnp.int32, (32, LANES), 1) < COEF

    @pl.loop(0, 16)
    def _(step):
        hot = one_hot_rows(cells_ref[step], GROUP)
        rows = both_halves(dot_nn(hot, table))
        for b in range(2 * GROUP):
            base = b * 64
            out_ref[step * 2 * GROUP + b] = jnp.where(
                left, rows[base : base + 32], rows[base + 32 : base + 64]
            )


def send_rows(multipoles, cells):
    return pl.pallas_call(
        send_kernel,
        name="send_rows",
        out_shape=jax.ShapeDtypeStruct((128, 32, LANES), F32),
        in_specs=[pl.BlockSpec(memory_space=pltpu.VMEM)] * 2,
        out_specs=pl.BlockSpec(memory_space=pltpu.VMEM),
        compiler_params=pltpu.CompilerParams(vmem_limit_bytes=VMEM_LIMIT),
    )(cells, multipoles)


def partner_kernel(
    index_a, index_b, targets_a, targets_b, ops_a, ops_b, multipoles_ref, local_ref, remote_ref, *scratch
):
    table, update_a, update_b = scratch[:3]
    banks = scratch[3:]
    step = pl.program_id(0)

    @pl.when(step == 0)
    def _():
        table[...] = cell_table(multipoles_ref[...]).astype(BF16)
        update_b[...] = jnp.zeros_like(update_b)
        for bank in banks:
            bank[...] = jnp.zeros_like(bank)

    def updates(targets, ops, out):
        hot = one_hot_rows(targets[0], GROUP)
        terms = dot_nn(hot, table[...]).astype(BF16)
        for i in range(GROUP):
            weights = operator_weights(ops[GROUP - 1 - i])
            out[i * LANES : (i + 1) * LANES, :] = dot_nt(terms[i * LANES : (i + 1) * LANES], weights)

    def scatter(index, update):
        for first in range(0, ROWS, BANKS):
            where = [index[0, (first + b) // LANES, (first + b) % LANES] for b in range(BANKS)]
            held = [banks[b][pl.ds(where[b], 1), :] for b in range(BANKS)]
            for b in range(BANKS):
                banks[b][pl.ds(where[b], 1), :] = held[b] + update[first + b : first + b + 1, :]

    updates(targets_a, ops_a, update_a)
    scatter(index_b, update_b)
    updates(targets_b, ops_b, update_b)
    scatter(index_a, update_a)

    @pl.when(step == pl.num_programs(0) - 1)
    def _():
        left = lax.broadcasted_iota(jnp.int32, (32, LANES), 1) < COEF

        def total(start, size):
            parts = [bank[pl.ds(start, size), :] for bank in banks]
            while len(parts) > 1:
                parts = [parts[i] + parts[i + 1] for i in range(0, len(parts), 2)]
            return both_halves(parts[0])

        @pl.loop(0, CELLS // 64)
        def _(i):
            start = pl.multiple_of(i * 64, 64)
            local_ref[pl.ds(start, 64), :] = total(start, 64)

        @pl.loop(0, 128)
        def _(i):
            rows = total(pl.multiple_of(CELLS + i * 64, 64), 64)
            remote_ref[i] = jnp.where(left, rows[:32], rows[32:])


def partner_sums(partners, targets, operators, multipoles):
    smem = functools.partial(pl.BlockSpec, (1, GROUP, LANES), memory_space=pltpu.SMEM)
    vmem = functools.partial(pl.BlockSpec, (1, GROUP, LANES))
    last = LIVE_GROUPS - 1
    return pl.pallas_call(
        partner_kernel,
        name="partner_sums",
        grid=(GROUPS // 2,),
        out_shape=(
            jax.ShapeDtypeStruct((CELLS, LANES), F32),
            jax.ShapeDtypeStruct((128, 32, LANES), F32),
        ),
        in_specs=[
            smem(lambda i: (2 * i, 0, 0)),
            smem(lambda i: (jnp.maximum(2 * i - 1, 0), 0, 0)),
            vmem(lambda i: (2 * i, 0, 0)),
            vmem(lambda i: (2 * i + 1, 0, 0)),
            pl.BlockSpec((GROUP, COEF, COEF), lambda i: (last - 2 * i, 0, 0)),
            pl.BlockSpec((GROUP, COEF, COEF), lambda i: (jnp.maximum(last - 1 - 2 * i, 0), 0, 0)),
            pl.BlockSpec((COEF, CELLS), lambda i: (0, 0)),
        ],
        out_specs=(
            pl.BlockSpec((CELLS, LANES), lambda i: (0, 0)),
            pl.BlockSpec((128, 32, LANES), lambda i: (0, 0, 0)),
        ),
        scratch_shapes=[
            pltpu.VMEM((CELLS, LANES), BF16),
            pltpu.VMEM((ROWS, LANES), F32),
            pltpu.VMEM((ROWS, LANES), F32),
        ]
        + [pltpu.VMEM((TABLE, LANES), F32)] * BANKS,
        compiler_params=pltpu.CompilerParams(
            dimension_semantics=("arbitrary",), vmem_limit_bytes=VMEM_LIMIT
        ),
        cost_estimate=pl.CostEstimate(
            flops=200_000_000_000, bytes_accessed=20_000_000, transcendentals=0
        ),
    )(partners, partners, targets, targets, operators, operators, multipoles)


def target_kernel(
    index_a, index_b, targets_a, targets_b, ops_a, ops_b, multipoles_ref, fetched_ref, out_ref, table, rows_a, rows_b
):
    step = pl.program_id(0)

    @pl.when(step == 0)
    def _():
        table[:CELLS, :] = cell_table(multipoles_ref[...])
        rows_b[...] = jnp.zeros_like(rows_b)
        out_ref[...] = jnp.zeros_like(out_ref)

        @pl.loop(0, 128)
        def _(i):
            table[pl.ds(pl.multiple_of(CELLS + i * 64, 64), 64), :] = unpack_rows(fetched_ref[i])

    def gather(index, rows):
        for r in range(ROWS):
            rows[r : r + 1, :] = table[pl.ds(index[0, r // LANES, r % LANES], 1), :]

    def accumulate(targets, ops, rows):
        updates = []
        for i in range(GROUP):
            weights = operator_weights(ops[i])
            updates.append(dot_nt(rows[i * LANES : (i + 1) * LANES, :].astype(BF16), weights))
        summed = both_halves(jnp.concatenate(updates, axis=0))
        hi = summed.astype(BF16).astype(F32)
        left = lax.broadcasted_iota(jnp.int32, summed.shape, 1) < COEF
        parts = jnp.where(left, hi, summed - hi).astype(BF16)
        out_ref[...] += dot_nn(one_hot_columns(targets[0], GROUP), parts)

    gather(index_a, rows_a)
    accumulate(targets_b, ops_b, rows_b)
    gather(index_b, rows_b)
    accumulate(targets_a, ops_a, rows_a)


def target_sums(partners, targets, operators, multipoles, fetched):
    smem = functools.partial(pl.BlockSpec, (1, GROUP, LANES), memory_space=pltpu.SMEM)
    vmem = functools.partial(pl.BlockSpec, (1, GROUP, LANES))
    last = LIVE_GROUPS - 1
    return pl.pallas_call(
        target_kernel,
        name="target_sums",
        grid=(GROUPS // 2,),
        out_shape=jax.ShapeDtypeStruct((CELLS, LANES), F32),
        in_specs=[
            smem(lambda i: (2 * i, 0, 0)),
            smem(lambda i: (2 * i + 1, 0, 0)),
            vmem(lambda i: (2 * i, 0, 0)),
            vmem(lambda i: (jnp.maximum(2 * i - 1, 0), 0, 0)),
            pl.BlockSpec((GROUP, COEF, COEF), lambda i: (2 * i, 0, 0)),
            pl.BlockSpec((GROUP, COEF, COEF), lambda i: (jnp.clip(2 * i - 1, 0, last), 0, 0)),
            pl.BlockSpec((COEF, CELLS), lambda i: (0, 0)),
            pl.BlockSpec((128, 32, LANES), lambda i: (0, 0, 0)),
        ],
        out_specs=pl.BlockSpec((CELLS, LANES), lambda i: (0, 0)),
        scratch_shapes=[
            pltpu.VMEM((TABLE, LANES), F32),
            pltpu.VMEM((ROWS, LANES), F32),
            pltpu.VMEM((ROWS, LANES), F32),
        ],
        compiler_params=pltpu.CompilerParams(
            dimension_semantics=("arbitrary",), vmem_limit_bytes=VMEM_LIMIT
        ),
        cost_estimate=pl.CostEstimate(
            flops=200_000_000_000, bytes_accessed=20_000_000, transcendentals=0
        ),
    )(partners, partners, targets, targets, operators, operators, multipoles, fetched)


def finish_kernel(cells_ref, returned_ref, parent_ref, partner_ref, target_ref, out_ref, total):
    total[...] = target_ref[...]

    @pl.loop(0, 16)
    def _(step):
        packed = returned_ref[pl.ds(step * 2 * GROUP, 2 * GROUP)]
        rows = unpack_rows(packed).reshape(ROWS, LANES).astype(BF16)
        total[...] += dot_nn(one_hot_columns(cells_ref[step], GROUP), rows)

    summed = both_halves(total[...]) + partner_ref[...]
    out_ref[...] = parent_ref[...] + summed.T[:COEF]


def finish(cells, returned, parent_locals, partner_part, target_part):
    return pl.pallas_call(
        finish_kernel,
        name="finish",
        out_shape=jax.ShapeDtypeStruct((COEF, CELLS), F32),
        in_specs=[pl.BlockSpec(memory_space=pltpu.VMEM)] * 5,
        out_specs=pl.BlockSpec(memory_space=pltpu.VMEM),
        scratch_shapes=[pltpu.VMEM((CELLS, LANES), F32)],
        compiler_params=pltpu.CompilerParams(vmem_limit_bytes=VMEM_LIMIT),
    )(cells, returned, parent_locals, partner_part, target_part)


def prepare(pair_target, pair_partner, pair_count, send_cells, send_count):
    position = lax.broadcasted_iota(jnp.int32, pair_target.shape, 1)
    targets = jnp.where(position < pair_count[0][:, None], pair_target, -1)
    targets = jnp.pad(targets, ((0, GROUP), (0, 0)), constant_values=-1)
    partners = jnp.pad(pair_partner, ((0, GROUP), (0, 0)))
    slot = lax.broadcasted_iota(jnp.int32, (128, 64), 1)
    cells = jnp.where(slot < send_count[0][:, None], send_cells[0].reshape(128, 64), -1)
    return (
        targets.reshape(GROUPS, GROUP, LANES),
        partners.reshape(GROUPS, GROUP, LANES),
        cells.reshape(16, GROUP, LANES),
    )


def shards(
    multipoles,
    parent_locals,
    operators,
    pair_target,
    pair_partner,
    pair_count,
    send_cells,
    send_count,
):
    axes = ("row", "col")
    targets, partners, cells = prepare(pair_target, pair_partner, pair_count, send_cells, send_count)
    outgoing = send_rows(multipoles, cells)
    fetched = lax.all_to_all(outgoing, axes, split_axis=0, concat_axis=0, tiled=True)
    partner_part, returning = partner_sums(partners, targets, operators, multipoles)
    returned = lax.all_to_all(returning, axes, split_axis=0, concat_axis=0, tiled=True)
    target_part = target_sums(partners, targets, operators, multipoles, fetched)
    return finish(cells, returned, parent_locals, partner_part, target_part)


def solution(mesh):
    in_specs = (
        P(None, ("row", "col")),
        P(None, ("row", "col")),
        P(),
        P(None, ("row", "col")),
        P(None, ("row", "col")),
        P(("row", "col"), None),
        P(("row", "col"), None),
        P(("row", "col"), None),
    )
    out_specs = P(None, ("row", "col"))
    return jax.shard_map(shards, mesh=mesh, in_specs=in_specs, out_specs=out_specs, check_vma=False)
```

```python
import jax
import jax.numpy as jnp
from jax import lax
from jax.experimental import pallas as pl
from jax.experimental.pallas import tpu as pltpu
from jax.sharding import PartitionSpec as P

F32 = jnp.float32
BF16 = jnp.bfloat16

COEF = 64
LANES = 128
CELLS = 1024
HALF = 512
REMOTE = 8192
TABLE = CELLS + REMOTE
OFFSETS = 316
SEGMENT = 8
ROWS = SEGMENT * LANES
STEPS = 20
PADDED = 320
DEAD = 0xFFFF
BANKS = 8
BATCH = 8
DEPTH = 4
WEAVE = False
MTILE = 256
VMEM_LIMIT = 60 * 1024 * 1024


def dot_nn(a, b):
    return lax.dot_general(a, b, (((1,), (0,)), ((), ())), preferred_element_type=F32)


def dot_nt(a, b):
    return lax.dot_general(a, b, (((1,), (1,)), ((), ())), preferred_element_type=F32)


def left_half(shape):
    return lax.broadcasted_iota(jnp.int32, shape, len(shape) - 1) < COEF


def both_halves(x):
    return x + pltpu.roll(x, COEF, 1)


def turn_operators(ops_ref, turned):
    @pl.loop(0, COEF // 2)
    def _(p):
        for start in range(0, OFFSETS, LANES):
            size = min(LANES, OFFSETS - start)
            pair = jnp.concatenate(
                [ops_ref[p, :, start : start + size], ops_ref[p + 32, :, start : start + size]], axis=0
            )
            turned[pl.ds(start * (COEF // 2) + p, size, stride=COEF // 2), :] = pair.T


def stage_operators(turned, staged, ks):
    size = COEF // 2
    for q, k in enumerate(ks):
        staged[q * size : (q + 1) * size, :] = turned[pl.ds(pl.multiple_of(k * size, size), size), :]


def weave(pieces, batches):
    done = 0
    for i, piece in enumerate(pieces):
        piece()
        until = (i + 1) * len(batches) // len(pieces)
        for batch in batches[done:until]:
            batch()
        done = until


def weight_pieces(staged, q, state):
    size = COEF // 2

    def doubled(x):
        left = left_half((size, LANES))
        swapped = pltpu.roll(x, COEF, 1)
        return [jnp.where(left, x, swapped), jnp.where(left, swapped, x)]

    def high():
        packed = staged[q * size : (q + 1) * size, :]
        hi = packed.astype(BF16).astype(F32)
        state["lo", q] = packed - hi
        state["hi", q] = doubled(hi)

    def low():
        parts = state.pop(("hi", q)) + doubled(state.pop(("lo", q)))
        state["w", q] = jnp.concatenate(parts, axis=0).astype(BF16)

    return [high, low]


def cell_table(multipoles):
    hi = multipoles.astype(BF16).astype(F32)
    lo = multipoles - hi
    return jnp.concatenate([hi, lo], axis=0).T


def folded_table(multipoles):
    table = cell_table(multipoles).astype(BF16)
    return jnp.concatenate([table[:HALF], table[HALF:]], axis=1)


def pair_codes(targets, counts, segment):
    first = segment * SEGMENT
    cells = targets[pl.ds(pl.multiple_of(jnp.maximum(first, 0), SEGMENT), SEGMENT), :]
    place = lax.broadcasted_iota(jnp.int32, (SEGMENT, LANES), 0)
    limit = jnp.zeros((SEGMENT, LANES), jnp.int32)
    for q in range(SEGMENT):
        k = first + q
        count = jnp.where((k >= 0) & (k < OFFSETS), counts[0, jnp.clip(k, 0, OFFSETS - 1)], 0)
        limit = jnp.where(place == q, count, limit)
    return fold(cells, lax.broadcasted_iota(jnp.int32, (SEGMENT, LANES), 1) < limit)


def slot_codes(cells_ref, counts, segment):
    cells = jnp.concatenate([cells_ref[2 * segment], cells_ref[2 * segment + 1]], axis=0)
    place = lax.broadcasted_iota(jnp.int32, (SEGMENT, LANES), 0)
    left = left_half((SEGMENT, LANES))
    limit = jnp.zeros((SEGMENT, LANES), jnp.int32)
    for q in range(SEGMENT):
        device = 2 * (segment * SEGMENT + q)
        limit = jnp.where(place == q, jnp.where(left, counts[0, device], counts[0, device + 1]), limit)
    return fold(cells, lax.broadcasted_iota(jnp.int32, (SEGMENT, LANES), 1) % 64 < limit)


def fold(cells, live):
    return jnp.where(live, (cells & (HALF - 1)) + ((cells >> 9) << 16), DEAD)


def spread_column(columns, q):
    code = jnp.broadcast_to(columns[:, q : q + 1], (LANES, LANES))
    lane = lax.broadcasted_iota(jnp.int32, (LANES, LANES), 1)
    low = code & DEAD
    hot = [(low == lane + start).astype(F32).astype(BF16) for start in range(0, HALF, LANES)]
    return jnp.concatenate(hot, axis=1), code > DEAD


def fetch_rows(columns, q, table, state):
    hot, upper = spread_column(columns, q)
    state["both", q] = dot_nn(hot, table[...])
    state["upper", q] = upper


def select_rows(q, state):
    part = state.pop(("both", q))
    return jnp.where(state.pop(("upper", q)), part[:, LANES:], part[:, :LANES])


def hot_columns(low, picks, start, size):
    cell = lax.broadcasted_iota(jnp.int32, (size, LANES), 0) + start
    hot = [(low[q : q + 1, :] == cell).astype(F32).astype(BF16) for q in picks]
    return jnp.concatenate(hot, axis=1)


def unpack_rows(packed):
    hi = packed.astype(BF16).astype(F32)
    lo = packed - hi
    left = left_half(packed.shape)
    axis = packed.ndim - 1
    first = jnp.where(left, hi, pltpu.roll(lo, COEF, axis))
    second = jnp.where(left, pltpu.roll(hi, COEF, axis), lo)
    return jnp.concatenate([first, second], axis=packed.ndim - 2)


def send_kernel(counts, cells_ref, multipoles_ref, out_ref, table):
    table[...] = folded_table(multipoles_ref[...])
    left = left_half((32, LANES))

    @pl.loop(0, 8)
    def _(segment):
        columns = slot_codes(cells_ref, counts, segment).T
        state = {}

        def store(q):
            rows = both_halves(select_rows(q, state))
            for b in range(2):
                base = b * 64
                out_ref[segment * 2 * SEGMENT + 2 * q + b] = jnp.where(
                    left, rows[base : base + 32], rows[base + 32 : base + 64]
                )

        for q in range(SEGMENT + 1):
            if q < SEGMENT:
                fetch_rows(columns, q, table, state)
            if q >= 1:
                store(q - 1)


SMEM_SPEC = pl.BlockSpec(memory_space=pltpu.SMEM)
VMEM_SPEC = pl.BlockSpec(memory_space=pltpu.VMEM)
HBM_SPEC = pl.BlockSpec(memory_space=pltpu.HBM)


def send_rows(counts, cells, multipoles):
    return pl.pallas_call(
        send_kernel,
        name="send_rows",
        out_shape=jax.ShapeDtypeStruct((128, 32, LANES), F32),
        in_specs=[SMEM_SPEC, VMEM_SPEC, VMEM_SPEC],
        out_specs=VMEM_SPEC,
        scratch_shapes=[pltpu.VMEM((HALF, 2 * LANES), BF16)],
        compiler_params=pltpu.CompilerParams(vmem_limit_bytes=VMEM_LIMIT),
    )(counts, cells, multipoles)


def fetch_index(partners, segment, index, sem):
    start = pl.multiple_of(jnp.clip(segment, 0, PADDED // SEGMENT - 1) * SEGMENT, SEGMENT)
    return pltpu.make_async_copy(partners.at[pl.ds(start, SEGMENT)], index, sem)


def load_pairs(partners_ref, targets_ref, partners, targets, sem_p, sem_t):
    copies = [
        pltpu.make_async_copy(partners_ref, partners.at[pl.ds(0, OFFSETS)], sem_p),
        pltpu.make_async_copy(targets_ref, targets.at[pl.ds(0, OFFSETS)], sem_t),
    ]
    for copy in copies:
        copy.start()
    for copy in copies:
        copy.wait()
    for pairs in (partners, targets):
        pairs[OFFSETS:, :] = jnp.zeros((PADDED - OFFSETS, LANES), jnp.int32)


def partner_kernel(
    counts,
    partners_ref,
    targets_ref,
    ops_ref,
    multipoles_ref,
    local_ref,
    remote_ref,
    turned_ref,
    native,
    table,
    *scratch,
):
    (turned, staged, partners, targets, update_a, update_b, index_e, index_o) = scratch[:8]
    sem_e, sem_o, sem_ops, sem_p, sem_t = scratch[8:13]
    banks = scratch[13:]

    load = pltpu.make_async_copy(ops_ref, native, sem_ops)
    load.start()
    load_pairs(partners_ref, targets_ref, partners, targets, sem_p, sem_t)
    fetch_index(partners, 0, index_e, sem_e).start()
    table[...] = folded_table(multipoles_ref[...])
    update_b[...] = jnp.zeros_like(update_b)

    @pl.loop(0, TABLE // 128)
    def _(i):
        for bank in banks:
            bank[pl.ds(pl.multiple_of(i * 128, 128), 128), :] = jnp.zeros((128, LANES), F32)

    load.wait()
    turn_operators(native, turned)
    keep = pltpu.make_async_copy(turned, turned_ref, sem_ops)
    keep.start()

    def update_pieces(columns, out):
        state = {}

        def store(q):
            rows = dot_nt(state.pop(("x", q)), state.pop(("w", q)))
            out[q * LANES : (q + 1) * LANES, :] = rows

        def select(q):
            state["x", q] = select_rows(q, state).astype(BF16)

        pieces = []
        for q in range(SEGMENT + 2):
            if q < SEGMENT:
                pieces.append(lambda q=q: fetch_rows(columns, q, table, state))
            if 1 <= q <= SEGMENT:
                pieces.extend(weight_pieces(staged, q - 1, state))
                pieces.append(lambda q=q: select(q - 1))
            if q >= 2:
                pieces.append(lambda q=q: store(q - 2))
        return pieces

    def scatter(index, update, first):
        rows = range(first, first + BANKS)
        where = [index[row // LANES, row % LANES] for row in rows]
        held = [banks[b][pl.ds(where[b], 1), :] for b in range(BANKS)]
        for b, row in enumerate(rows):
            banks[b][pl.ds(where[b], 1), :] = held[b] + update[row : row + 1, :]

    def both(segment, out, index, update):
        columns = pair_codes(targets, counts, segment).T
        first = OFFSETS - 1 - segment * SEGMENT
        stage_operators(turned, staged, [jnp.maximum(first - q, 0) for q in range(SEGMENT)])
        pieces = update_pieces(columns, out)
        batches = [lambda i=i: scatter(index, update, i) for i in range(0, ROWS, BANKS)]
        if WEAVE:
            weave(pieces, batches)
        else:
            weave(pieces, [])
            weave([lambda: None], batches)

    @pl.loop(0, STEPS)
    def _(step):
        fetch_index(partners, 2 * step - 1, index_e, sem_e).wait()
        fetch_index(partners, 2 * step, index_o, sem_o).start()
        both(2 * step, update_a, index_e, update_b)
        fetch_index(partners, 2 * step, index_o, sem_o).wait()
        fetch_index(partners, 2 * step + 1, index_e, sem_e).start()
        both(2 * step + 1, update_b, index_o, update_a)

    fetch_index(partners, 2 * STEPS - 1, index_e, sem_e).wait()
    for first in range(0, OFFSETS % SEGMENT * LANES, BANKS):
        scatter(index_e, update_b, first)

    left = left_half((32, LANES))

    def total(start, size):
        parts = [bank[pl.ds(start, size), :] for bank in banks]
        while len(parts) > 1:
            parts = [
                parts[i] + parts[i + 1] if i + 1 < len(parts) else parts[i]
                for i in range(0, len(parts), 2)
            ]
        return both_halves(parts[0])

    @pl.loop(0, CELLS // 256)
    def _(i):
        for j in range(4):
            start = pl.multiple_of(i * 256 + j * 64, 64)
            local_ref[pl.ds(start, 64), :] = total(start, 64)

    @pl.loop(0, 32)
    def _(i):
        for j in range(4):
            rows = total(pl.multiple_of(CELLS + i * 256 + j * 64, 64), 64)
            remote_ref[4 * i + j] = jnp.where(left, rows[:32], rows[32:])

    keep.wait()


def pair_scratch():
    return [
        pltpu.VMEM((COEF // 2 * OFFSETS, LANES), F32),
        pltpu.VMEM((COEF // 2 * SEGMENT, LANES), F32),
        pltpu.VMEM((PADDED, LANES), jnp.int32),
        pltpu.VMEM((PADDED, LANES), jnp.int32),
        pltpu.VMEM((ROWS, LANES), F32),
        pltpu.VMEM((ROWS, LANES), F32),
        pltpu.SMEM((SEGMENT, LANES), jnp.int32),
        pltpu.SMEM((SEGMENT, LANES), jnp.int32),
    ] + [pltpu.SemaphoreType.DMA] * 5


def partner_sums(counts, partners, targets, operators, multipoles):
    return pl.pallas_call(
        partner_kernel,
        name="partner_sums",
        out_shape=(
            jax.ShapeDtypeStruct((CELLS, LANES), F32),
            jax.ShapeDtypeStruct((128, 32, LANES), F32),
            jax.ShapeDtypeStruct((COEF // 2 * OFFSETS, LANES), F32),
        ),
        in_specs=[SMEM_SPEC, HBM_SPEC, HBM_SPEC, HBM_SPEC, VMEM_SPEC],
        out_specs=(VMEM_SPEC, VMEM_SPEC, HBM_SPEC),
        scratch_shapes=[
            pltpu.VMEM((COEF, COEF, OFFSETS), F32),
            pltpu.VMEM((HALF, 2 * LANES), BF16),
        ]
        + pair_scratch()
        + [pltpu.VMEM((TABLE, LANES), F32)] * BANKS,
        compiler_params=pltpu.CompilerParams(vmem_limit_bytes=VMEM_LIMIT),
        cost_estimate=pl.CostEstimate(
            flops=200_000_000_000, bytes_accessed=20_000_000, transcendentals=0
        ),
    )(counts, partners, targets, operators, multipoles)


def target_kernel(
    counts,
    partners_ref,
    targets_ref,
    turned_ref,
    multipoles_ref,
    fetched_ref,
    out_ref,
    table,
    total,
    *scratch,
):
    (turned, staged, partners, targets, rows_a, rows_b, index_e, index_o) = scratch[:8]
    sem_e, sem_o, sem_ops, sem_p, sem_t = scratch[8:]

    load = pltpu.make_async_copy(turned_ref, turned, sem_ops)
    load.start()
    load_pairs(partners_ref, targets_ref, partners, targets, sem_p, sem_t)
    fetch_index(partners, 0, index_e, sem_e).start()
    table[:CELLS, :] = cell_table(multipoles_ref[...])
    rows_b[...] = jnp.zeros_like(rows_b)
    total[...] = jnp.zeros_like(total)

    @pl.loop(0, 32)
    def _(i):
        for j in range(4):
            start = pl.multiple_of(CELLS + (4 * i + j) * 64, 64)
            table[pl.ds(start, 64), :] = unpack_rows(fetched_ref[4 * i + j])

    load.wait()

    def gather(index, rows, start, stop):
        for r in range(start, stop):
            rows[r : r + 1, :] = table[pl.ds(index[r // LANES, r % LANES], 1), :]

    def stage(segment):
        first = segment * SEGMENT
        ks = [jnp.clip(first + q, 0, OFFSETS - 1) for q in range(SEGMENT)]
        stage_operators(turned, staged, ks)
        return pair_codes(targets, counts, segment)

    def sum_pieces(codes, rows, count):
        state = {}
        low = codes & DEAD

        def product(q):
            x = rows[q * LANES : (q + 1) * LANES, :].astype(BF16)
            state["u", q] = dot_nt(state.pop(("w", q)), x)

        def add_halves(q):
            both = state.pop(("u", q))
            summed = both[:COEF] + both[COEF:]
            hi = summed.astype(BF16).astype(F32)
            state["v", q] = jnp.concatenate([hi, summed - hi], axis=0)

        def spread(q):
            upper = jnp.broadcast_to(codes[q : q + 1, :], (LANES, LANES)) > DEAD
            part = state.pop(("v", q))
            state["s", q] = jnp.concatenate(
                [jnp.where(upper, 0.0, part), jnp.where(upper, part, 0.0)], axis=0
            ).astype(BF16)

        def collect(p, start):
            picks = range(p * DEPTH, (p + 1) * DEPTH)
            spreads = jnp.concatenate([state["s", q] for q in picks], axis=1)
            total[start : start + MTILE, :] += dot_nt(hot_columns(low, picks, start, MTILE), spreads)

        pieces = []
        for q in range(count + 2):
            if q < count:
                pieces.extend(weight_pieces(staged, q, state))
                pieces.append(lambda q=q: product(q))
            if 1 <= q <= count:
                pieces.append(lambda q=q: add_halves(q - 1))
                pieces.append(lambda q=q: spread(q - 1))
            if q >= 2 and (q - 1) % DEPTH == 0:
                for start in range(0, HALF, MTILE):
                    pieces.append(lambda p=(q - 2) // DEPTH, start=start: collect(p, start))
        return pieces

    def both(segment, done, index, rows):
        codes = stage(segment)
        weave(
            sum_pieces(codes, done, SEGMENT),
            [lambda i=i: gather(index, rows, i, i + BATCH) for i in range(0, ROWS, BATCH)],
        )

    @pl.loop(0, STEPS)
    def _(step):
        fetch_index(partners, 2 * step, index_e, sem_e).wait()
        fetch_index(partners, 2 * step + 1, index_o, sem_o).start()
        both(2 * step - 1, rows_b, index_e, rows_a)
        fetch_index(partners, 2 * step + 1, index_o, sem_o).wait()
        fetch_index(partners, 2 * step + 2, index_e, sem_e).start()
        both(2 * step, rows_a, index_o, rows_b)

    fetch_index(partners, 2 * STEPS, index_e, sem_e).wait()
    weave(sum_pieces(stage(2 * STEPS - 1), rows_b, OFFSETS % SEGMENT), [])
    out_ref[...] = total[...]


def target_sums(counts, partners, targets, turned, multipoles, fetched):
    return pl.pallas_call(
        target_kernel,
        name="target_sums",
        out_shape=jax.ShapeDtypeStruct((HALF, 2 * LANES), F32),
        in_specs=[SMEM_SPEC, HBM_SPEC, HBM_SPEC, HBM_SPEC, VMEM_SPEC, VMEM_SPEC],
        out_specs=VMEM_SPEC,
        scratch_shapes=[
            pltpu.VMEM((TABLE, LANES), F32),
            pltpu.VMEM((HALF, 2 * LANES), F32),
        ]
        + pair_scratch(),
        compiler_params=pltpu.CompilerParams(vmem_limit_bytes=VMEM_LIMIT),
        cost_estimate=pl.CostEstimate(
            flops=200_000_000_000, bytes_accessed=20_000_000, transcendentals=0
        ),
    )(counts, partners, targets, turned, multipoles, fetched)


def finish_kernel(
    counts, cells_ref, returned_ref, parent_ref, partner_ref, target_ref, out_ref, total
):
    total[...] = target_ref[...]

    @pl.loop(0, 8)
    def _(segment):
        codes = slot_codes(cells_ref, counts, segment)
        columns = codes.T
        spreads = []
        for q in range(SEGMENT):
            packed = returned_ref[pl.ds(segment * 2 * SEGMENT + 2 * q, 2)]
            rows = unpack_rows(packed).reshape(LANES, LANES)
            upper = jnp.broadcast_to(columns[:, q : q + 1], (LANES, LANES)) > DEAD
            spreads.append(
                jnp.concatenate(
                    [jnp.where(upper, 0.0, rows), jnp.where(upper, rows, 0.0)], axis=1
                ).astype(BF16)
            )
        hot = hot_columns(codes & DEAD, range(SEGMENT), 0, HALF)
        total[...] += dot_nn(hot, jnp.concatenate(spreads, axis=0))

    for half in range(2):
        summed = both_halves(total[:, half * LANES : (half + 1) * LANES])
        summed = summed + partner_ref[half * HALF : (half + 1) * HALF]
        columns = slice(half * HALF, (half + 1) * HALF)
        out_ref[:, columns] = parent_ref[:, columns] + summed.T[:COEF]


def finish(counts, cells, returned, parent_locals, partner_part, target_part):
    return pl.pallas_call(
        finish_kernel,
        name="finish",
        out_shape=jax.ShapeDtypeStruct((COEF, CELLS), F32),
        in_specs=[SMEM_SPEC] + [VMEM_SPEC] * 5,
        out_specs=VMEM_SPEC,
        scratch_shapes=[pltpu.VMEM((HALF, 2 * LANES), F32)],
        compiler_params=pltpu.CompilerParams(vmem_limit_bytes=VMEM_LIMIT),
    )(counts, cells, returned, parent_locals, partner_part, target_part)


def shards(
    multipoles,
    parent_locals,
    operators,
    pair_target,
    pair_partner,
    pair_count,
    send_cells,
    send_count,
):
    axes = ("row", "col")
    cells = send_cells.reshape(16, 4, LANES)
    ops = operators.transpose(1, 2, 0)
    outgoing = send_rows(send_count, cells, multipoles)
    fetched = exchange(outgoing, axes)
    partner_part, returning, turned = partner_sums(
        pair_count, pair_partner, pair_target, ops, multipoles
    )
    returned = exchange(returning, axes)
    target_part = target_sums(pair_count, pair_partner, pair_target, turned, multipoles, fetched)
    return finish(send_count, cells, returned, parent_locals, partner_part, target_part)


def exchange(blocks, axes):
    return lax.all_to_all(blocks, axes, split_axis=0, concat_axis=0, tiled=True)


def solution(mesh):
    in_specs = (
        P(None, ("row", "col")),
        P(None, ("row", "col")),
        P(),
        P(None, ("row", "col")),
        P(None, ("row", "col")),
        P(("row", "col"), None),
        P(("row", "col"), None),
        P(("row", "col"), None),
    )
    out_specs = P(None, ("row", "col"))
    return jax.shard_map(shards, mesh=mesh, in_specs=in_specs, out_specs=out_specs, check_vma=False)
```

```python
import jax
import jax.numpy as jnp
from jax import lax
from jax.experimental import pallas as pl
from jax.experimental.pallas import tpu as pltpu
from jax.sharding import PartitionSpec as P

F32 = jnp.float32
BF16 = jnp.bfloat16

COEF = 64
LANES = 128
CELLS = 1024
HALF = 512
REMOTE = 8192
TABLE = CELLS + REMOTE
OFFSETS = 316
SEGMENT = 8
ROWS = SEGMENT * LANES
STEPS = 20
PADDED = 320
DEAD = 0xFFFF
BANKS = 4
FDEPTH = 4
FSEGMENTS = 4
TURN = 8
PITCH = 33
BATCH = 8
DEPTH = 4
WEAVE = False
MTILE = 256
VMEM_LIMIT = 60 * 1024 * 1024


def dot_nn(a, b):
    return lax.dot_general(a, b, (((1,), (0,)), ((), ())), preferred_element_type=F32)


def dot_nt(a, b):
    return lax.dot_general(a, b, (((1,), (1,)), ((), ())), preferred_element_type=F32)


def left_half(shape):
    return lax.broadcasted_iota(jnp.int32, shape, len(shape) - 1) < COEF


def both_halves(x):
    return x + pltpu.roll(x, COEF, 1)


def turn_operators(ops_ref, turned):
    @pl.loop(0, COEF // 2 // TURN)
    def _(i):
        for t in range(TURN):
            p = i * TURN + t
            for start in range(0, OFFSETS, LANES):
                size = min(LANES, OFFSETS - start)
                lanes = slice(start, start + size)
                pair = jnp.concatenate([ops_ref[p, :, lanes], ops_ref[p + 32, :, lanes]], axis=0)
                turned[pl.ds(start * PITCH + p, size, stride=PITCH), :] = pair.T


def stage_operators(turned, staged, ks):
    size = COEF // 2
    for q, k in enumerate(ks):
        staged[q * size : (q + 1) * size, :] = turned[pl.ds(k * PITCH, size), :]


def weave(pieces, batches):
    done = 0
    for i, piece in enumerate(pieces):
        piece()
        until = (i + 1) * len(batches) // len(pieces)
        for batch in batches[done:until]:
            batch()
        done = until


def weight_pieces(staged, q, state):
    size = COEF // 2

    def doubled(x):
        left = left_half((size, LANES))
        swapped = pltpu.roll(x, COEF, 1)
        return [jnp.where(left, x, swapped), jnp.where(left, swapped, x)]

    def high():
        packed = staged[q * size : (q + 1) * size, :]
        hi = packed.astype(BF16).astype(F32)
        state["lo", q] = packed - hi
        state["hi", q] = doubled(hi)

    def low():
        parts = state.pop(("hi", q)) + doubled(state.pop(("lo", q)))
        state["w", q] = jnp.concatenate(parts, axis=0).astype(BF16)

    return [high, low]


def cell_table(multipoles):
    hi = multipoles.astype(BF16).astype(F32)
    lo = multipoles - hi
    return jnp.concatenate([hi, lo], axis=0).T


def folded_table(multipoles):
    hi, lo = multipoles.astype(BF16), multipoles - multipoles.astype(BF16).astype(F32)
    both = jnp.concatenate([hi, lo.astype(BF16)], axis=0)
    return jnp.concatenate([both[:, :HALF], both[:, HALF:]], axis=0)


def pair_codes(targets, counts, segment):
    first = segment * SEGMENT
    cells = targets[pl.ds(pl.multiple_of(jnp.maximum(first, 0), SEGMENT), SEGMENT), :]
    place = lax.broadcasted_iota(jnp.int32, (SEGMENT, LANES), 0)
    limit = jnp.zeros((SEGMENT, LANES), jnp.int32)
    for q in range(SEGMENT):
        k = first + q
        count = jnp.where((k >= 0) & (k < OFFSETS), counts[0, jnp.clip(k, 0, OFFSETS - 1)], 0)
        limit = jnp.where(place == q, count, limit)
    return fold(cells, lax.broadcasted_iota(jnp.int32, (SEGMENT, LANES), 1) < limit)


def slot_codes(cells_ref, counts, segment):
    cells = jnp.concatenate([cells_ref[2 * segment], cells_ref[2 * segment + 1]], axis=0)
    place = lax.broadcasted_iota(jnp.int32, (SEGMENT, LANES), 0)
    left = left_half((SEGMENT, LANES))
    limit = jnp.zeros((SEGMENT, LANES), jnp.int32)
    for q in range(SEGMENT):
        device = 2 * (segment * SEGMENT + q)
        limit = jnp.where(place == q, jnp.where(left, counts[0, device], counts[0, device + 1]), limit)
    return fold(cells, lax.broadcasted_iota(jnp.int32, (SEGMENT, LANES), 1) % 64 < limit)


def fold(cells, live):
    return jnp.where(live, (cells & (HALF - 1)) + ((cells >> 9) << 16), DEAD)


def fetch_columns(codes, picks, table, state):
    both = dot_nn(table[...], hot_columns(codes & DEAD, picks, 0, HALF))
    for i, q in enumerate(picks):
        state["both", q] = both[:, i * LANES : (i + 1) * LANES]


def select_columns(codes, q, state):
    part = state.pop(("both", q))
    upper = jnp.broadcast_to(codes[q : q + 1, :], (LANES, LANES)) > DEAD
    return jnp.where(upper, part[LANES:], part[:LANES])


def hot_columns(low, picks, start, size):
    cell = lax.broadcasted_iota(jnp.int32, (size, LANES), 0) + start
    hot = [(low[q : q + 1, :] == cell).astype(F32).astype(BF16) for q in picks]
    return jnp.concatenate(hot, axis=1)


def pack_columns(columns):
    left = left_half((32, LANES))
    top, bottom = columns[:32], columns[32:]
    return (
        jnp.where(left, top, pltpu.roll(bottom, COEF, 1)),
        jnp.where(left, pltpu.roll(top, COEF, 1), bottom),
    )


def unpack_columns(first, second):
    left = left_half((32, LANES))
    return [
        jnp.where(left, first, pltpu.roll(second, COEF, 1)),
        jnp.where(left, pltpu.roll(first, COEF, 1), second),
    ]


def hi_lo(x):
    hi = x.astype(BF16).astype(F32)
    return jnp.concatenate([hi, x - hi], axis=0)


def spread_codes(codes, q, part):
    upper = jnp.broadcast_to(codes[q : q + 1, :], (LANES, LANES)) > DEAD
    return jnp.concatenate(
        [jnp.where(upper, 0.0, part), jnp.where(upper, part, 0.0)], axis=0
    ).astype(BF16)


def unpack_rows(packed):
    hi = packed.astype(BF16).astype(F32)
    lo = packed - hi
    left = left_half(packed.shape)
    axis = packed.ndim - 1
    first = jnp.where(left, hi, pltpu.roll(lo, COEF, axis))
    second = jnp.where(left, pltpu.roll(hi, COEF, axis), lo)
    return jnp.concatenate([first, second], axis=packed.ndim - 2)


def send_kernel(counts, cells_ref, multipoles_ref, out_ref, table):
    table[...] = folded_table(multipoles_ref[...])
    left = left_half((32, LANES))

    @pl.loop(0, 8)
    def _(segment):
        codes = slot_codes(cells_ref, counts, segment)
        state = {}

        def store(q):
            x = select_columns(codes, q, state)
            x = x[:COEF] + x[COEF:]
            rows = jnp.concatenate([x, x], axis=0).T
            for b in range(2):
                base = b * 64
                out_ref[segment * 2 * SEGMENT + 2 * q + b] = jnp.where(
                    left, rows[base : base + 32], rows[base + 32 : base + 64]
                )

        for q in range(0, SEGMENT + 2, 2):
            if q < SEGMENT:
                fetch_columns(codes, range(q, q + 2), table, state)
            if q >= 2:
                store(q - 2)
                store(q - 1)


SMEM_SPEC = pl.BlockSpec(memory_space=pltpu.SMEM)
VMEM_SPEC = pl.BlockSpec(memory_space=pltpu.VMEM)
HBM_SPEC = pl.BlockSpec(memory_space=pltpu.HBM)


def send_rows(counts, cells, multipoles):
    return pl.pallas_call(
        send_kernel,
        name="send_rows",
        out_shape=jax.ShapeDtypeStruct((128, 32, LANES), F32),
        in_specs=[SMEM_SPEC, VMEM_SPEC, VMEM_SPEC],
        out_specs=VMEM_SPEC,
        scratch_shapes=[pltpu.VMEM((2 * LANES, HALF), BF16)],
        compiler_params=pltpu.CompilerParams(vmem_limit_bytes=VMEM_LIMIT),
    )(counts, cells, multipoles)


def fetch_index(partners, segment, index, sem):
    start = pl.multiple_of(jnp.clip(segment, 0, PADDED // SEGMENT - 1) * SEGMENT, SEGMENT)
    return pltpu.make_async_copy(partners.at[pl.ds(start, SEGMENT)], index, sem)


def load_pairs(partners_ref, targets_ref, partners, targets, sem_p, sem_t):
    copies = [
        pltpu.make_async_copy(partners_ref, partners.at[pl.ds(0, OFFSETS)], sem_p),
        pltpu.make_async_copy(targets_ref, targets.at[pl.ds(0, OFFSETS)], sem_t),
    ]
    for copy in copies:
        copy.start()
    return copies


def finish_pairs(copies, partners, targets):
    for copy in copies:
        copy.wait()
    for pairs in (partners, targets):
        pairs[OFFSETS:, :] = jnp.zeros((PADDED - OFFSETS, LANES), jnp.int32)


def partner_kernel(
    counts,
    partners_ref,
    targets_ref,
    ops_ref,
    multipoles_ref,
    local_ref,
    remote_ref,
    turned_ref,
    native,
    table,
    *scratch,
):
    (turned, staged, partners, targets, update_a, update_b, index_e, index_o) = scratch[:8]
    sem_e, sem_o, sem_ops, sem_p, sem_t = scratch[8:13]
    banks = scratch[13:]

    load = pltpu.make_async_copy(ops_ref, native, sem_ops)
    load.start()
    pairs = load_pairs(partners_ref, targets_ref, partners, targets, sem_p, sem_t)
    table[...] = folded_table(multipoles_ref[...])
    update_a[...] = jnp.zeros_like(update_a)
    update_b[...] = jnp.zeros_like(update_b)

    @pl.loop(0, TABLE // 128)
    def _(i):
        for bank in banks:
            bank[pl.ds(pl.multiple_of(i * 128, 128), 128), :] = jnp.zeros((128, LANES), F32)

    finish_pairs(pairs, partners, targets)
    fetch_index(partners, 0, index_e, sem_e).start()
    load.wait()
    turn_operators(native, turned)
    keep = pltpu.make_async_copy(turned, turned_ref, sem_ops)
    keep.start()

    def update_pieces(codes, out):
        state = {}

        def product(q):
            both = dot_nn(state.pop(("w", q)), state.pop(("x", q)))
            state["u", q] = both[:COEF] + both[COEF:]

        def store(q):
            pair = jnp.concatenate([state.pop(("u", q)), state.pop(("u", q + 1))], axis=0)
            out[q // 2 * LANES : (q // 2 + 1) * LANES, :] = pair.T

        def select(q):
            state["x", q] = select_columns(codes, q, state).astype(BF16)

        pieces = []
        for q in range(0, SEGMENT + 4, 2):
            if q < SEGMENT:
                pieces.append(lambda q=q: fetch_columns(codes, range(q, q + 2), table, state))
            for r in (q - 2, q - 1):
                if 0 <= r < SEGMENT:
                    pieces.extend(weight_pieces(staged, r, state))
                    pieces.append(lambda r=r: select(r))
            for r in (q - 4, q - 3):
                if r >= 0:
                    pieces.append(lambda r=r: product(r))
            if q >= 4:
                pieces.append(lambda q=q: store(q - 4))
        return pieces

    def scatter(index, update, first):
        rows = range(first, first + BANKS)
        left = left_half((1, LANES))
        parts = []
        for side, mask in ((0, left), (1, ~left)):
            for bank, row in zip(banks, rows):
                where = index[row // LANES * 2 + side, row % LANES]
                view = bank.at[pl.ds(where, 1), :]
                parts.append((view, mask, view[...], row))
        for view, mask, held, row in parts:
            pltpu.store(view, held + update[row : row + 1, :], mask=mask)

    def both(segment, out, index, update):
        codes = pair_codes(targets, counts, segment)
        first = OFFSETS - 1 - segment * SEGMENT
        stage_operators(turned, staged, [jnp.maximum(first - q, 0) for q in range(SEGMENT)])
        pieces = update_pieces(codes, out)
        batches = [lambda i=i: scatter(index, update, i) for i in range(0, ROWS // 2, BANKS)]
        if WEAVE:
            weave(pieces, batches)
        else:
            weave(pieces, [])
            weave([lambda: None], batches)

    @pl.loop(0, STEPS)
    def _(step):
        fetch_index(partners, 2 * step - 1, index_e, sem_e).wait()
        fetch_index(partners, 2 * step, index_o, sem_o).start()
        both(2 * step, update_a, index_e, update_b)
        fetch_index(partners, 2 * step, index_o, sem_o).wait()
        fetch_index(partners, 2 * step + 1, index_e, sem_e).start()
        both(2 * step + 1, update_b, index_o, update_a)

    fetch_index(partners, 2 * STEPS - 1, index_e, sem_e).wait()
    for first in range(0, OFFSETS % SEGMENT * LANES // 2, BANKS):
        scatter(index_e, update_b, first)

    def total(start, size):
        parts = [bank[pl.ds(start, size), :] for bank in banks]
        while len(parts) > 1:
            parts = [
                parts[i] + parts[i + 1] if i + 1 < len(parts) else parts[i]
                for i in range(0, len(parts), 2)
            ]
        return parts[0]

    @pl.loop(0, CELLS // 256)
    def _(i):
        start = pl.multiple_of(i * 256, 256)
        local_ref[pl.ds(start, 256), :] = both_halves(total(start, 256))

    @pl.loop(0, 16)
    def _(i):
        for j in range(4):
            both = total(pl.multiple_of(CELLS + i * 512 + j * LANES, LANES), LANES).T
            first, second = pack_columns(both[:COEF] + both[COEF:])
            remote_ref[8 * i + 2 * j] = first
            remote_ref[8 * i + 2 * j + 1] = second

    keep.wait()


def pair_scratch():
    return [
        pltpu.VMEM((PITCH * OFFSETS, LANES), F32),
        pltpu.VMEM((COEF // 2 * SEGMENT, LANES), F32),
        pltpu.VMEM((PADDED, LANES), jnp.int32),
        pltpu.VMEM((PADDED, LANES), jnp.int32),
        pltpu.VMEM((ROWS, LANES), F32),
        pltpu.VMEM((ROWS, LANES), F32),
        pltpu.SMEM((SEGMENT, LANES), jnp.int32),
        pltpu.SMEM((SEGMENT, LANES), jnp.int32),
    ] + [pltpu.SemaphoreType.DMA] * 5


def partner_sums(counts, partners, targets, operators, multipoles):
    return pl.pallas_call(
        partner_kernel,
        name="partner_sums",
        out_shape=(
            jax.ShapeDtypeStruct((CELLS, LANES), F32),
            jax.ShapeDtypeStruct((128, 32, LANES), F32),
            jax.ShapeDtypeStruct((PITCH * OFFSETS, LANES), F32),
        ),
        in_specs=[SMEM_SPEC, HBM_SPEC, HBM_SPEC, HBM_SPEC, VMEM_SPEC],
        out_specs=(VMEM_SPEC, VMEM_SPEC, HBM_SPEC),
        scratch_shapes=[
            pltpu.VMEM((COEF, COEF, OFFSETS), F32),
            pltpu.VMEM((2 * LANES, HALF), BF16),
        ]
        + pair_scratch()
        + [pltpu.VMEM((TABLE, LANES), F32)] * BANKS,
        compiler_params=pltpu.CompilerParams(vmem_limit_bytes=VMEM_LIMIT),
        cost_estimate=pl.CostEstimate(
            flops=200_000_000_000, bytes_accessed=20_000_000, transcendentals=0
        ),
    )(counts, partners, targets, operators, multipoles)


def target_kernel(
    counts,
    partners_ref,
    targets_ref,
    turned_ref,
    multipoles_ref,
    fetched_ref,
    out_ref,
    table,
    total,
    *scratch,
):
    (turned, staged, partners, targets, rows_a, rows_b, index_e, index_o) = scratch[:8]
    sem_e, sem_o, sem_ops, sem_p, sem_t = scratch[8:]

    load = pltpu.make_async_copy(turned_ref, turned, sem_ops)
    load.start()
    pairs = load_pairs(partners_ref, targets_ref, partners, targets, sem_p, sem_t)
    table[:CELLS, :] = cell_table(multipoles_ref[...])
    rows_b[...] = jnp.zeros_like(rows_b)
    total[...] = jnp.zeros_like(total)

    @pl.loop(0, 32)
    def _(i):
        for j in range(4):
            start = pl.multiple_of(CELLS + (4 * i + j) * 64, 64)
            table[pl.ds(start, 64), :] = unpack_rows(fetched_ref[4 * i + j])

    finish_pairs(pairs, partners, targets)
    fetch_index(partners, 0, index_e, sem_e).start()
    load.wait()

    def gather(index, rows, start, stop):
        for r in range(start, stop):
            rows[r : r + 1, :] = table[pl.ds(index[r // LANES, r % LANES], 1), :]

    def stage(segment):
        first = segment * SEGMENT
        ks = [jnp.clip(first + q, 0, OFFSETS - 1) for q in range(SEGMENT)]
        stage_operators(turned, staged, ks)
        return pair_codes(targets, counts, segment)

    def sum_pieces(codes, rows, count):
        state = {}
        low = codes & DEAD

        def product(q):
            x = rows[q * LANES : (q + 1) * LANES, :].astype(BF16)
            state["u", q] = dot_nt(state.pop(("w", q)), x)

        def add_halves(q):
            both = state.pop(("u", q))
            state["v", q] = hi_lo(both[:COEF] + both[COEF:])

        def spread(q):
            state["s", q] = spread_codes(codes, q, state.pop(("v", q)))

        def collect(p, start):
            picks = range(p * DEPTH, (p + 1) * DEPTH)
            spreads = jnp.concatenate([state["s", q] for q in picks], axis=1)
            total[start : start + MTILE, :] += dot_nt(hot_columns(low, picks, start, MTILE), spreads)

        pieces = []
        for q in range(count + 2):
            if q < count:
                pieces.extend(weight_pieces(staged, q, state))
                pieces.append(lambda q=q: product(q))
            if 1 <= q <= count:
                pieces.append(lambda q=q: add_halves(q - 1))
                pieces.append(lambda q=q: spread(q - 1))
            if q >= 2 and (q - 1) % DEPTH == 0:
                for start in range(0, HALF, MTILE):
                    pieces.append(lambda p=(q - 2) // DEPTH, start=start: collect(p, start))
        return pieces

    def both(segment, done, index, rows):
        codes = stage(segment)
        weave(
            sum_pieces(codes, done, SEGMENT),
            [lambda i=i: gather(index, rows, i, i + BATCH) for i in range(0, ROWS, BATCH)],
        )

    @pl.loop(0, STEPS)
    def _(step):
        fetch_index(partners, 2 * step, index_e, sem_e).wait()
        fetch_index(partners, 2 * step + 1, index_o, sem_o).start()
        both(2 * step - 1, rows_b, index_e, rows_a)
        fetch_index(partners, 2 * step + 1, index_o, sem_o).wait()
        fetch_index(partners, 2 * step + 2, index_e, sem_e).start()
        both(2 * step, rows_a, index_o, rows_b)

    fetch_index(partners, 2 * STEPS, index_e, sem_e).wait()
    weave(sum_pieces(stage(2 * STEPS - 1), rows_b, OFFSETS % SEGMENT), [])
    out_ref[...] = total[...]


def target_sums(counts, partners, targets, turned, multipoles, fetched):
    return pl.pallas_call(
        target_kernel,
        name="target_sums",
        out_shape=jax.ShapeDtypeStruct((HALF, 2 * LANES), F32),
        in_specs=[SMEM_SPEC, HBM_SPEC, HBM_SPEC, HBM_SPEC, VMEM_SPEC, VMEM_SPEC],
        out_specs=VMEM_SPEC,
        scratch_shapes=[
            pltpu.VMEM((TABLE, LANES), F32),
            pltpu.VMEM((HALF, 2 * LANES), F32),
        ]
        + pair_scratch(),
        compiler_params=pltpu.CompilerParams(vmem_limit_bytes=VMEM_LIMIT),
        cost_estimate=pl.CostEstimate(
            flops=200_000_000_000, bytes_accessed=20_000_000, transcendentals=0
        ),
    )(counts, partners, targets, turned, multipoles, fetched)


def finish_kernel(
    counts, cells_ref, returned_ref, parent_ref, partner_ref, target_ref, out_ref, total
):
    total[...] = target_ref[...]

    def prepare(codes, segment, picks):
        spreads = []
        for q in picks:
            block = segment * 2 * SEGMENT + 2 * q
            columns = unpack_columns(returned_ref[block], returned_ref[block + 1])
            spreads.append(spread_codes(codes, q, hi_lo(jnp.concatenate(columns, axis=0))))
        return jnp.concatenate(spreads, axis=1)

    @pl.loop(0, 8 // FSEGMENTS)
    def _(trip):
        segments = [trip * FSEGMENTS + i for i in range(FSEGMENTS)]
        codes = [slot_codes(cells_ref, counts, segment) for segment in segments]
        chunks = [
            (i, range(p, p + FDEPTH)) for i in range(FSEGMENTS) for p in range(0, SEGMENT, FDEPTH)
        ]
        ready = prepare(codes[0], segments[0], chunks[0][1])
        for n, (i, picks) in enumerate(chunks):
            spreads = ready
            if n + 1 < len(chunks):
                j, ahead = chunks[n + 1]
                ready = prepare(codes[j], segments[j], ahead)
            for start in range(0, HALF, MTILE):
                hot = hot_columns(codes[i] & DEAD, picks, start, MTILE)
                total[start : start + MTILE, :] += dot_nt(hot, spreads)

    for half in range(2):
        summed = both_halves(total[:, half * LANES : (half + 1) * LANES])
        summed = summed + partner_ref[half * HALF : (half + 1) * HALF]
        columns = slice(half * HALF, (half + 1) * HALF)
        out_ref[:, columns] = parent_ref[:, columns] + summed.T[:COEF]


def finish(counts, cells, returned, parent_locals, partner_part, target_part):
    return pl.pallas_call(
        finish_kernel,
        name="finish",
        out_shape=jax.ShapeDtypeStruct((COEF, CELLS), F32),
        in_specs=[SMEM_SPEC] + [VMEM_SPEC] * 5,
        out_specs=VMEM_SPEC,
        scratch_shapes=[pltpu.VMEM((HALF, 2 * LANES), F32)],
        compiler_params=pltpu.CompilerParams(vmem_limit_bytes=VMEM_LIMIT),
    )(counts, cells, returned, parent_locals, partner_part, target_part)


def shards(
    multipoles,
    parent_locals,
    operators,
    pair_target,
    pair_partner,
    pair_count,
    send_cells,
    send_count,
):
    axes = ("row", "col")
    cells = send_cells.reshape(16, 4, LANES)
    ops = operators.transpose(1, 2, 0)
    outgoing = send_rows(send_count, cells, multipoles)
    fetched = exchange(outgoing, axes)
    partner_part, returning, turned = partner_sums(
        pair_count, pair_partner, pair_target, ops, multipoles
    )
    returned = exchange(returning, axes)
    target_part = target_sums(pair_count, pair_partner, pair_target, turned, multipoles, fetched)
    return finish(send_count, cells, returned, parent_locals, partner_part, target_part)


def exchange(blocks, axes):
    return lax.all_to_all(blocks, axes, split_axis=0, concat_axis=0, tiled=True)


def solution(mesh):
    in_specs = (
        P(None, ("row", "col")),
        P(None, ("row", "col")),
        P(),
        P(None, ("row", "col")),
        P(None, ("row", "col")),
        P(("row", "col"), None),
        P(("row", "col"), None),
        P(("row", "col"), None),
    )
    out_specs = P(None, ("row", "col"))
    return jax.shard_map(shards, mesh=mesh, in_specs=in_specs, out_specs=out_specs, check_vma=False)
```

```python
import jax
import jax.numpy as jnp
from jax import lax
from jax.experimental import pallas as pl
from jax.experimental.pallas import tpu as pltpu
from jax.sharding import PartitionSpec as P

F32 = jnp.float32
BF16 = jnp.bfloat16

COEF = 64
LANES = 128
CELLS = 1024
HALF = 512
REMOTE = 8192
TABLE = CELLS + REMOTE
OFFSETS = 316
SEGMENT = 8
ROWS = SEGMENT * LANES
SEGMENTS = 40
PARTNER_SPAN = 4
TARGET_SPAN = 2
PADDED = 320
DEAD = 0xFFFF
BANKS = 4
FDEPTH = 4
FSEGMENTS = 4
TURN = 8
PITCH = 33
BATCH = 8
DEPTH = 2
WEAVE = False
MTILE = 256
VMEM_LIMIT = 60 * 1024 * 1024


def dot_nn(a, b):
    return lax.dot_general(a, b, (((1,), (0,)), ((), ())), preferred_element_type=F32)


def dot_nt(a, b):
    return lax.dot_general(a, b, (((1,), (1,)), ((), ())), preferred_element_type=F32)


def left_half(shape):
    return lax.broadcasted_iota(jnp.int32, shape, len(shape) - 1) < COEF


def both_halves(x):
    return x + pltpu.roll(x, COEF, 1)


def turn_operators(ops_ref, turned):
    @pl.loop(0, COEF // 2 // TURN)
    def _(i):
        for t in range(TURN):
            p = i * TURN + t
            for start in range(0, OFFSETS, LANES):
                size = min(LANES, OFFSETS - start)
                lanes = slice(start, start + size)
                pair = jnp.concatenate([ops_ref[p, :, lanes], ops_ref[p + 32, :, lanes]], axis=0)
                turned[pl.ds(start * PITCH + p, size, stride=PITCH), :] = pair.T


def stage_operators(turned, staged, ks):
    size = COEF // 2
    for q, k in enumerate(ks):
        staged[q * size : (q + 1) * size, :] = turned[pl.ds(k * PITCH, size), :]


def weave(pieces, batches):
    done = 0
    for i, piece in enumerate(pieces):
        piece()
        until = (i + 1) * len(batches) // len(pieces)
        for batch in batches[done:until]:
            batch()
        done = until


def weight_pieces(staged, q, state):
    size = COEF // 2

    def doubled(x):
        left = left_half((size, LANES))
        swapped = pltpu.roll(x, COEF, 1)
        return [jnp.where(left, x, swapped), jnp.where(left, swapped, x)]

    def high():
        packed = staged[q * size : (q + 1) * size, :]
        hi = packed.astype(BF16).astype(F32)
        state["lo", q] = packed - hi
        state["hi", q] = doubled(hi)

    def low():
        parts = state.pop(("hi", q)) + doubled(state.pop(("lo", q)))
        state["w", q] = jnp.concatenate(parts, axis=0).astype(BF16)

    return [high, low]


def cell_table(multipoles):
    hi = multipoles.astype(BF16).astype(F32)
    lo = multipoles - hi
    return jnp.concatenate([hi, lo], axis=0).T


def folded_table(multipoles):
    hi, lo = multipoles.astype(BF16), multipoles - multipoles.astype(BF16).astype(F32)
    both = jnp.concatenate([hi, lo.astype(BF16)], axis=0)
    return jnp.concatenate([both[:, :HALF], both[:, HALF:]], axis=0)


def pair_codes(targets, counts, segment):
    first = segment * SEGMENT
    cells = targets[pl.ds(pl.multiple_of(jnp.maximum(first, 0), SEGMENT), SEGMENT), :]
    place = lax.broadcasted_iota(jnp.int32, (SEGMENT, LANES), 0)
    limit = jnp.zeros((SEGMENT, LANES), jnp.int32)
    for q in range(SEGMENT):
        k = first + q
        count = jnp.where((k >= 0) & (k < OFFSETS), counts[0, jnp.clip(k, 0, OFFSETS - 1)], 0)
        limit = jnp.where(place == q, count, limit)
    return fold(cells, lax.broadcasted_iota(jnp.int32, (SEGMENT, LANES), 1) < limit)


def slot_codes(cells_ref, counts, segment):
    cells = jnp.concatenate([cells_ref[2 * segment], cells_ref[2 * segment + 1]], axis=0)
    place = lax.broadcasted_iota(jnp.int32, (SEGMENT, LANES), 0)
    left = left_half((SEGMENT, LANES))
    limit = jnp.zeros((SEGMENT, LANES), jnp.int32)
    for q in range(SEGMENT):
        device = 2 * (segment * SEGMENT + q)
        limit = jnp.where(place == q, jnp.where(left, counts[0, device], counts[0, device + 1]), limit)
    return fold(cells, lax.broadcasted_iota(jnp.int32, (SEGMENT, LANES), 1) % 64 < limit)


def fold(cells, live):
    return jnp.where(live, (cells & (HALF - 1)) + ((cells >> 9) << 16), DEAD)


def fetch_columns(codes, picks, table, state):
    both = dot_nn(table[...], hot_columns(codes & DEAD, picks, 0, HALF))
    for i, q in enumerate(picks):
        state["both", q] = both[:, i * LANES : (i + 1) * LANES]


def select_columns(codes, q, state):
    part = state.pop(("both", q))
    upper = jnp.broadcast_to(codes[q : q + 1, :], (LANES, LANES)) > DEAD
    return jnp.where(upper, part[LANES:], part[:LANES])


def hot_columns(low, picks, start, size):
    cell = lax.broadcasted_iota(jnp.int32, (size, LANES), 0) + start
    hot = [(low[q : q + 1, :] == cell).astype(F32).astype(BF16) for q in picks]
    return jnp.concatenate(hot, axis=1)


def pack_columns(columns):
    left = left_half((32, LANES))
    top, bottom = columns[:32], columns[32:]
    return (
        jnp.where(left, top, pltpu.roll(bottom, COEF, 1)),
        jnp.where(left, pltpu.roll(top, COEF, 1), bottom),
    )


def unpack_columns(first, second):
    left = left_half((32, LANES))
    return [
        jnp.where(left, first, pltpu.roll(second, COEF, 1)),
        jnp.where(left, pltpu.roll(first, COEF, 1), second),
    ]


def hi_lo(x):
    hi = x.astype(BF16).astype(F32)
    return jnp.concatenate([hi, x - hi], axis=0)


def spread_codes(codes, q, part):
    upper = jnp.broadcast_to(codes[q : q + 1, :], (LANES, LANES)) > DEAD
    return jnp.concatenate(
        [jnp.where(upper, 0.0, part), jnp.where(upper, part, 0.0)], axis=0
    ).astype(BF16)


def unpack_rows(packed):
    hi = packed.astype(BF16).astype(F32)
    lo = packed - hi
    left = left_half(packed.shape)
    axis = packed.ndim - 1
    first = jnp.where(left, hi, pltpu.roll(lo, COEF, axis))
    second = jnp.where(left, pltpu.roll(hi, COEF, axis), lo)
    return jnp.concatenate([first, second], axis=packed.ndim - 2)


def send_kernel(counts, cells_ref, multipoles_ref, out_ref, table):
    table[...] = folded_table(multipoles_ref[...])
    left = left_half((32, LANES))

    state = {}

    def store(codes, segment, q):
        x = select_columns(codes, q, state)
        x = x[:COEF] + x[COEF:]
        rows = jnp.concatenate([x, x], axis=0).T
        for b in range(2):
            base = b * 64
            out_ref[segment * 2 * SEGMENT + 2 * q + b] = jnp.where(
                left, rows[base : base + 32], rows[base + 32 : base + 64]
            )

    @pl.loop(0, 8 // FSEGMENTS)
    def _(trip):
        segments = [trip * FSEGMENTS + i for i in range(FSEGMENTS)]
        codes = [slot_codes(cells_ref, counts, segment) for segment in segments]
        chunks = [(i, q) for i in range(FSEGMENTS) for q in range(0, SEGMENT, 2)]
        for n in range(len(chunks) + 1):
            if n > 0:
                j, r = chunks[n - 1]
                store(codes[j], segments[j], r)
            if n < len(chunks):
                i, q = chunks[n]
                held = state.pop(("both", chunks[n - 1][1] + 1), None) if n > 0 else None
                fetch_columns(codes[i], range(q, q + 2), table, state)
                if held is not None:
                    state["both", r + 1] = held
            if n > 0:
                store(codes[j], segments[j], r + 1)


SMEM_SPEC = pl.BlockSpec(memory_space=pltpu.SMEM)
VMEM_SPEC = pl.BlockSpec(memory_space=pltpu.VMEM)
HBM_SPEC = pl.BlockSpec(memory_space=pltpu.HBM)


def send_rows(counts, cells, multipoles):
    return pl.pallas_call(
        send_kernel,
        name="send_rows",
        out_shape=jax.ShapeDtypeStruct((128, 32, LANES), F32),
        in_specs=[SMEM_SPEC, VMEM_SPEC, VMEM_SPEC],
        out_specs=VMEM_SPEC,
        scratch_shapes=[pltpu.VMEM((2 * LANES, HALF), BF16)],
        compiler_params=pltpu.CompilerParams(vmem_limit_bytes=VMEM_LIMIT),
    )(counts, cells, multipoles)


def fetch_index(partners, segment, index, sem):
    start = (jnp.clip(segment, -1, PADDED // SEGMENT - 1) + 1) * SEGMENT
    rows = pl.ds(pl.multiple_of(start, SEGMENT), index.shape[0])
    return pltpu.make_async_copy(partners.at[rows], index, sem)


def load_pairs(partners_ref, targets_ref, partners, targets, sem_p, sem_t):
    copies = [
        pltpu.make_async_copy(partners_ref, partners.at[pl.ds(SEGMENT, OFFSETS)], sem_p),
        pltpu.make_async_copy(targets_ref, targets.at[pl.ds(0, OFFSETS)], sem_t),
    ]
    for copy in copies:
        copy.start()
    return copies


def finish_pairs(copies, partners, targets):
    for copy in copies:
        copy.wait()
    targets[OFFSETS:, :] = jnp.zeros((PADDED - OFFSETS, LANES), jnp.int32)
    partners[:SEGMENT, :] = jnp.zeros((SEGMENT, LANES), jnp.int32)
    rest = partners.shape[0] - SEGMENT - OFFSETS
    partners[SEGMENT + OFFSETS :, :] = jnp.zeros((rest, LANES), jnp.int32)


def partner_kernel(
    counts,
    partners_ref,
    targets_ref,
    ops_ref,
    multipoles_ref,
    local_ref,
    remote_ref,
    turned_ref,
    native,
    table,
    *scratch,
):
    (turned, staged, partners, targets, update_a, update_b, index_e, index_o) = scratch[:8]
    sem_e, sem_o, sem_ops, sem_p, sem_t = scratch[8:13]
    banks = scratch[13:]

    load = pltpu.make_async_copy(ops_ref, native, sem_ops)
    load.start()
    pairs = load_pairs(partners_ref, targets_ref, partners, targets, sem_p, sem_t)
    table[...] = folded_table(multipoles_ref[...])
    update_a[...] = jnp.zeros_like(update_a)
    update_b[...] = jnp.zeros_like(update_b)

    @pl.loop(0, TABLE // 128)
    def _(i):
        for bank in banks:
            bank[pl.ds(pl.multiple_of(i * 128, 128), 128), :] = jnp.zeros((128, LANES), F32)

    finish_pairs(pairs, partners, targets)
    fetch_index(partners, -1, index_e, sem_e).start()
    load.wait()
    turn_operators(native, turned)
    keep = pltpu.make_async_copy(turned, turned_ref, sem_ops)
    keep.start()

    def update_pieces(codes, out):
        state = {}

        def product(q):
            both = dot_nn(state.pop(("w", q)), state.pop(("x", q)))
            state["u", q] = both[:COEF] + both[COEF:]

        def store(q):
            pair = jnp.concatenate([state.pop(("u", q)), state.pop(("u", q + 1))], axis=0)
            out[q // 2 * LANES : (q // 2 + 1) * LANES, :] = pair.T

        def select(q):
            state["x", q] = select_columns(codes, q, state).astype(BF16)

        pieces = []
        for q in range(0, SEGMENT + 4, 2):
            if q < SEGMENT:
                pieces.append(lambda q=q: fetch_columns(codes, range(q, q + 2), table, state))
            for r in (q - 2, q - 1):
                if 0 <= r < SEGMENT:
                    pieces.extend(weight_pieces(staged, r, state))
                    pieces.append(lambda r=r: select(r))
            for r in (q - 4, q - 3):
                if r >= 0:
                    pieces.append(lambda r=r: product(r))
            if q >= 4:
                pieces.append(lambda q=q: store(q - 4))
        return pieces

    def scatter(index, base, update, first):
        rows = range(first, first + BANKS)
        left = left_half((1, LANES))
        parts = []
        for side, mask in ((0, left), (1, ~left)):
            for bank, row in zip(banks, rows):
                where = index[base + row // LANES * 2 + side, row % LANES]
                view = bank.at[pl.ds(where, 1), :]
                parts.append((view, mask, view[...], row))
        for view, mask, held, row in parts:
            pltpu.store(view, held + update[row : row + 1, :], mask=mask)

    def both(segment, out, index, base, update):
        codes = pair_codes(targets, counts, segment)
        first = OFFSETS - 1 - segment * SEGMENT
        stage_operators(turned, staged, [jnp.maximum(first - q, 0) for q in range(SEGMENT)])
        pieces = update_pieces(codes, out)
        batches = [lambda i=i: scatter(index, base, update, i) for i in range(0, ROWS // 2, BANKS)]
        if WEAVE:
            weave(pieces, batches)
        else:
            weave(pieces, [])
            weave([lambda: None], batches)

    buffers = (update_a, update_b)

    @pl.loop(0, SEGMENTS // (2 * PARTNER_SPAN))
    def _(step):
        first = 2 * PARTNER_SPAN * step
        fetch_index(partners, first - 1, index_e, sem_e).wait()
        fetch_index(partners, first + PARTNER_SPAN - 1, index_o, sem_o).start()
        for i in range(PARTNER_SPAN):
            both(first + i, buffers[i % 2], index_e, i * SEGMENT, buffers[1 - i % 2])
        fetch_index(partners, first + PARTNER_SPAN - 1, index_o, sem_o).wait()
        fetch_index(partners, first + 2 * PARTNER_SPAN - 1, index_e, sem_e).start()
        for i in range(PARTNER_SPAN):
            both(first + PARTNER_SPAN + i, buffers[i % 2], index_o, i * SEGMENT, buffers[1 - i % 2])

    fetch_index(partners, SEGMENTS - 1, index_e, sem_e).wait()
    for first in range(0, OFFSETS % SEGMENT * LANES // 2, BANKS):
        scatter(index_e, 0, update_b, first)

    def total(start, size):
        parts = [bank[pl.ds(start, size), :] for bank in banks]
        while len(parts) > 1:
            parts = [
                parts[i] + parts[i + 1] if i + 1 < len(parts) else parts[i]
                for i in range(0, len(parts), 2)
            ]
        return parts[0]

    @pl.loop(0, CELLS // 256)
    def _(i):
        start = pl.multiple_of(i * 256, 256)
        local_ref[pl.ds(start, 256), :] = both_halves(total(start, 256))

    @pl.loop(0, 16)
    def _(i):
        for j in range(4):
            both = total(pl.multiple_of(CELLS + i * 512 + j * LANES, LANES), LANES).T
            first, second = pack_columns(both[:COEF] + both[COEF:])
            remote_ref[8 * i + 2 * j] = first
            remote_ref[8 * i + 2 * j + 1] = second

    keep.wait()


def pair_scratch(span):
    return [
        pltpu.VMEM((PITCH * OFFSETS, LANES), F32),
        pltpu.VMEM((COEF // 2 * SEGMENT, LANES), F32),
        pltpu.VMEM((PADDED + span * SEGMENT, LANES), jnp.int32),
        pltpu.VMEM((PADDED, LANES), jnp.int32),
        pltpu.VMEM((ROWS, LANES), F32),
        pltpu.VMEM((ROWS, LANES), F32),
        pltpu.SMEM((span * SEGMENT, LANES), jnp.int32),
        pltpu.SMEM((span * SEGMENT, LANES), jnp.int32),
    ] + [pltpu.SemaphoreType.DMA] * 5


def partner_sums(counts, partners, targets, operators, multipoles):
    return pl.pallas_call(
        partner_kernel,
        name="partner_sums",
        out_shape=(
            jax.ShapeDtypeStruct((CELLS, LANES), F32),
            jax.ShapeDtypeStruct((128, 32, LANES), F32),
            jax.ShapeDtypeStruct((PITCH * OFFSETS, LANES), F32),
        ),
        in_specs=[SMEM_SPEC, HBM_SPEC, HBM_SPEC, HBM_SPEC, VMEM_SPEC],
        out_specs=(VMEM_SPEC, VMEM_SPEC, HBM_SPEC),
        scratch_shapes=[
            pltpu.VMEM((COEF, COEF, OFFSETS), F32),
            pltpu.VMEM((2 * LANES, HALF), BF16),
        ]
        + pair_scratch(PARTNER_SPAN)
        + [pltpu.VMEM((TABLE, LANES), F32)] * BANKS,
        compiler_params=pltpu.CompilerParams(vmem_limit_bytes=VMEM_LIMIT),
        cost_estimate=pl.CostEstimate(
            flops=200_000_000_000, bytes_accessed=20_000_000, transcendentals=0
        ),
    )(counts, partners, targets, operators, multipoles)


def target_kernel(
    counts,
    partners_ref,
    targets_ref,
    turned_ref,
    multipoles_ref,
    fetched_ref,
    out_ref,
    table,
    total,
    *scratch,
):
    (turned, staged, partners, targets, rows_a, rows_b, index_e, index_o) = scratch[:8]
    sem_e, sem_o, sem_ops, sem_p, sem_t = scratch[8:]

    load = pltpu.make_async_copy(turned_ref, turned, sem_ops)
    load.start()
    pairs = load_pairs(partners_ref, targets_ref, partners, targets, sem_p, sem_t)
    table[:CELLS, :] = cell_table(multipoles_ref[...])
    rows_b[...] = jnp.zeros_like(rows_b)
    total[...] = jnp.zeros_like(total)

    @pl.loop(0, 32)
    def _(i):
        for j in range(4):
            start = pl.multiple_of(CELLS + (4 * i + j) * 64, 64)
            table[pl.ds(start, 64), :] = unpack_rows(fetched_ref[4 * i + j])

    finish_pairs(pairs, partners, targets)
    fetch_index(partners, 0, index_e, sem_e).start()
    load.wait()

    def gather(index, base, rows, start, stop):
        for r in range(start, stop):
            rows[r : r + 1, :] = table[pl.ds(index[base + r // LANES, r % LANES], 1), :]

    def stage(segment):
        first = segment * SEGMENT
        ks = [jnp.clip(first + q, 0, OFFSETS - 1) for q in range(SEGMENT)]
        stage_operators(turned, staged, ks)
        return pair_codes(targets, counts, segment)

    def sum_pieces(codes, rows, count):
        state = {}
        low = codes & DEAD

        def product(q):
            x = rows[q * LANES : (q + 1) * LANES, :].astype(BF16)
            state["u", q] = dot_nt(state.pop(("w", q)), x)

        def add_halves(q):
            both = state.pop(("u", q))
            state["v", q] = hi_lo(both[:COEF] + both[COEF:])

        def spread(q):
            state["s", q] = spread_codes(codes, q, state.pop(("v", q)))

        def collect(p, start):
            picks = range(p * DEPTH, (p + 1) * DEPTH)
            spreads = jnp.concatenate([state["s", q] for q in picks], axis=1)
            total[start : start + MTILE, :] += dot_nt(hot_columns(low, picks, start, MTILE), spreads)

        pieces = []
        for q in range(count + 2):
            if q < count:
                pieces.extend(weight_pieces(staged, q, state))
                pieces.append(lambda q=q: product(q))
            if 1 <= q <= count:
                pieces.append(lambda q=q: add_halves(q - 1))
                pieces.append(lambda q=q: spread(q - 1))
            if q >= 2 and (q - 1) % DEPTH == 0:
                for start in range(0, HALF, MTILE):
                    pieces.append(lambda p=(q - 2) // DEPTH, start=start: collect(p, start))
        return pieces

    def both(segment, done, index, base, rows):
        codes = stage(segment)
        weave(
            sum_pieces(codes, done, SEGMENT),
            [lambda i=i: gather(index, base, rows, i, i + BATCH) for i in range(0, ROWS, BATCH)],
        )

    buffers = (rows_a, rows_b)

    @pl.loop(0, SEGMENTS // (2 * TARGET_SPAN))
    def _(step):
        first = 2 * TARGET_SPAN * step
        fetch_index(partners, first, index_e, sem_e).wait()
        fetch_index(partners, first + TARGET_SPAN, index_o, sem_o).start()
        for i in range(TARGET_SPAN):
            both(first + i - 1, buffers[1 - i % 2], index_e, i * SEGMENT, buffers[i % 2])
        fetch_index(partners, first + TARGET_SPAN, index_o, sem_o).wait()
        fetch_index(partners, first + 2 * TARGET_SPAN, index_e, sem_e).start()
        for i in range(TARGET_SPAN):
            both(first + TARGET_SPAN + i - 1, buffers[1 - i % 2], index_o, i * SEGMENT, buffers[i % 2])

    fetch_index(partners, SEGMENTS, index_e, sem_e).wait()
    weave(sum_pieces(stage(SEGMENTS - 1), rows_b, OFFSETS % SEGMENT), [])
    out_ref[...] = total[...]


def target_sums(counts, partners, targets, turned, multipoles, fetched):
    return pl.pallas_call(
        target_kernel,
        name="target_sums",
        out_shape=jax.ShapeDtypeStruct((HALF, 2 * LANES), F32),
        in_specs=[SMEM_SPEC, HBM_SPEC, HBM_SPEC, HBM_SPEC, VMEM_SPEC, VMEM_SPEC],
        out_specs=VMEM_SPEC,
        scratch_shapes=[
            pltpu.VMEM((TABLE, LANES), F32),
            pltpu.VMEM((HALF, 2 * LANES), F32),
        ]
        + pair_scratch(TARGET_SPAN),
        compiler_params=pltpu.CompilerParams(vmem_limit_bytes=VMEM_LIMIT),
        cost_estimate=pl.CostEstimate(
            flops=200_000_000_000, bytes_accessed=20_000_000, transcendentals=0
        ),
    )(counts, partners, targets, turned, multipoles, fetched)


def finish_kernel(
    counts, cells_ref, returned_ref, parent_ref, partner_ref, target_ref, out_ref, total
):
    total[...] = target_ref[...]

    def prepare(codes, segment, picks):
        spreads = []
        for q in picks:
            block = segment * 2 * SEGMENT + 2 * q
            columns = unpack_columns(returned_ref[block], returned_ref[block + 1])
            spreads.append(spread_codes(codes, q, hi_lo(jnp.concatenate(columns, axis=0))))
        return jnp.concatenate(spreads, axis=1)

    @pl.loop(0, 8 // FSEGMENTS)
    def _(trip):
        segments = [trip * FSEGMENTS + i for i in range(FSEGMENTS)]
        codes = [slot_codes(cells_ref, counts, segment) for segment in segments]
        chunks = [
            (i, range(p, p + FDEPTH)) for i in range(FSEGMENTS) for p in range(0, SEGMENT, FDEPTH)
        ]
        ready = prepare(codes[0], segments[0], chunks[0][1])
        for n, (i, picks) in enumerate(chunks):
            spreads = ready
            if n + 1 < len(chunks):
                j, ahead = chunks[n + 1]
                ready = prepare(codes[j], segments[j], ahead)
            for start in range(0, HALF, MTILE):
                hot = hot_columns(codes[i] & DEAD, picks, start, MTILE)
                total[start : start + MTILE, :] += dot_nt(hot, spreads)

    for half in range(2):
        summed = both_halves(total[:, half * LANES : (half + 1) * LANES])
        summed = summed + partner_ref[half * HALF : (half + 1) * HALF]
        columns = slice(half * HALF, (half + 1) * HALF)
        out_ref[:, columns] = parent_ref[:, columns] + summed.T[:COEF]


def finish(counts, cells, returned, parent_locals, partner_part, target_part):
    return pl.pallas_call(
        finish_kernel,
        name="finish",
        out_shape=jax.ShapeDtypeStruct((COEF, CELLS), F32),
        in_specs=[SMEM_SPEC] + [VMEM_SPEC] * 5,
        out_specs=VMEM_SPEC,
        scratch_shapes=[pltpu.VMEM((HALF, 2 * LANES), F32)],
        compiler_params=pltpu.CompilerParams(vmem_limit_bytes=VMEM_LIMIT),
    )(counts, cells, returned, parent_locals, partner_part, target_part)


def shards(
    multipoles,
    parent_locals,
    operators,
    pair_target,
    pair_partner,
    pair_count,
    send_cells,
    send_count,
):
    axes = ("row", "col")
    cells = send_cells.reshape(16, 4, LANES)
    ops = operators.transpose(1, 2, 0)
    outgoing = send_rows(send_count, cells, multipoles)
    fetched = exchange(outgoing, axes)
    partner_part, returning, turned = partner_sums(
        pair_count, pair_partner, pair_target, ops, multipoles
    )
    returned = exchange(returning, axes)
    target_part = target_sums(pair_count, pair_partner, pair_target, turned, multipoles, fetched)
    return finish(send_count, cells, returned, parent_locals, partner_part, target_part)


def exchange(blocks, axes):
    return lax.all_to_all(blocks, axes, split_axis=0, concat_axis=0, tiled=True)


def solution(mesh):
    in_specs = (
        P(None, ("row", "col")),
        P(None, ("row", "col")),
        P(),
        P(None, ("row", "col")),
        P(None, ("row", "col")),
        P(("row", "col"), None),
        P(("row", "col"), None),
        P(("row", "col"), None),
    )
    out_specs = P(None, ("row", "col"))
    return jax.shard_map(shards, mesh=mesh, in_specs=in_specs, out_specs=out_specs, check_vma=False)
```
